256 devices in a mesh: wide: 32 (over y, x, core), batch: 8 (over z).
Axes of the slice: x: 4, y: 4, z: 8, core: 2. Of those that a mesh axis runs over, the one named last changes fastest.
Arguments:
- q_latent: bfloat16 [8, 64, 4, 1536], P('batch', 'wide'), may hold values from -6 to 6
- draft_start: int32 [8, 64], P('batch', 'wide'), may hold values from 4096 to 8191
- cache_len: int32 [8, 64], P('batch', 'wide'), may hold values from 1 to 4092, 163680 in all within a row
- latent_cache: bfloat16 [8, 64, 4096, 576], P('batch', 'wide'), may hold values from -576 to 576
- w_q_up: bfloat16 [1536, 24576], P('batch', 'wide'), may hold values from -0.15625 to 0.15625
- w_k_absorb: bfloat16 [128, 128, 512], P('wide'), may hold values from -0.5 to 0.5
- value_up_weight: bfloat16 [128, 512, 128], P('wide'), may hold values from -0.25 to 0.25
Outputs:
- values: bfloat16 [8, 64, 4, 16384], P('batch', None, None, 'wide')
The draws below stay inside these ranges and needn't reach their ends.
All inputs are finite; a program needn't handle non-finite values. No bound on the sum of `cache_len` on one device may be relied on, other than what follows from the above.
Results may differ from the reference program's by a relative error of at most 0.014.
The reference program's roundings to bfloat16 on the way count: a program that leaves them out, or rounds other values in their place, can miss the bound.
Values may be sent and summed in bfloat16 or wider, within the bound.
No kernel may reach another device: no remote copies, remote signals or barrier semaphores. Data moves between devices by JAX's collectives and lax.ppermute only.
A program may use at most 128 MiB of HBM per device.

```python
import math
import jax
import jax.numpy as jnp
import numpy as np
from jax import lax

QL = 1536
HEADS = 128
NOPE = 128
ROPE = 64
KVL = 512
VD = 128
DRAFT = 4
CTX = 4096
REQUESTS_GROUP = 64
GROUPS = 8


def draw_latent_cache(key, part):
    base = 1.5 * jax.random.truncated_normal(key, -6.0, 6.0, (GROUPS, REQUESTS_GROUP, CTX, KVL + ROPE), jnp.float32)
    return base.astype(jnp.bfloat16)


def plant(entries, rng, smallest, high):
    index_at = [jax.random.randint(jax.random.fold_in(rng, axis), (), 0, length) for axis, length in enumerate(entries.shape)]
    longest = entries.shape.index(max(entries.shape))
    beside = index_at[:longest] + [(index_at[longest] + 1) % entries.shape[longest]] + index_at[longest + 1:]
    return entries.at[tuple(index_at)].set(smallest).at[tuple(beside)].set(high)


def steps_of(stream_key, shape, shards, smallest, high):
    level, own = 1.0, jax.random.fold_in(stream_key, 6)
    for position, shards_of in shards:
        draws = jnp.exp(jax.random.uniform(jax.random.fold_in(own, position), (shards_of,), jnp.float32, smallest / len(shards), high / len(shards)))
        level = level * jnp.repeat(draws, shape[position] // shards_of).reshape([-1 if axis == position else 1 for axis in range(len(shape))])
    return level


def profile(number_of, total, bound, skew):
    loads = [(1 << 20) // math.isqrt(rank ** skew) + 1 for rank in range(2, number_of + 1)]
    surplus, holding = total - bound - (number_of - 1), [1] * (number_of - 1)
    while surplus > 0:
        free = [i for i in range(number_of - 1) if holding[i] < bound]
        pool, budget = sum([loads[i] for i in free]), surplus
        for i in free:
            more = min(bound - holding[i], max(1, budget * loads[i] // pool), surplus)
            holding[i] = holding[i] + more
            surplus = surplus - more
    return np.array([bound] + holding)


def ragged_sizes(stream_key, number_of, total, most, slope):
    if number_of == 2:
        one = jax.random.randint(stream_key, (), max(1, total - most), min(most, total - 1) + 1)
        return jnp.stack([one, total - one])
    sizes = jnp.asarray(profile(number_of, total, most, slope), jnp.int32)
    twos = (number_of - 1) // 2
    giver, sink = sizes[1:1 + 2 * twos:2], sizes[2:2 + 2 * twos:2]
    margin = jnp.minimum(giver - 1, most - sink)
    shifted = jax.random.randint(jax.random.fold_in(stream_key, 1), (twos,), 0, 1 << 20) % (margin + 1)
    sizes = sizes.at[1:1 + 2 * twos:2].set(giver - shifted).at[2:2 + 2 * twos:2].set(sink + shifted)
    return sizes[jax.random.permutation(jax.random.fold_in(stream_key, 2), number_of)]


def normal_values(rng, dims, deviation, reach, shards=(), held_as=jnp.bfloat16):
    gain = steps_of(rng, dims, shards, -0.22, 0.18) if shards else 1.0
    entries = jax.random.normal(rng, dims, jnp.float32) * deviation * gain
    return jnp.minimum(jnp.maximum(entries, -reach), reach).astype(held_as)


def setup_inputs(seed: int = 0) -> dict:
    keys = jax.random.split(jax.random.key(seed), 8)
    q_latent = normal_values(keys[0], (GROUPS, REQUESTS_GROUP, DRAFT, QL), 1.0, 6.0, ((0, 8), (1, 32)))
    draft_start = plant(jax.random.randint(keys[1], (GROUPS, REQUESTS_GROUP), CTX, 2 * CTX), jax.random.fold_in(keys[1], 1), CTX, (2 * CTX) - 1).astype(jnp.int32)
    cache_len = jax.vmap(lambda own: ragged_sizes(own, REQUESTS_GROUP, REQUESTS_GROUP * (CTX - DRAFT) * 5 // 8, CTX - DRAFT, 2))(jax.random.split(keys[2], GROUPS)).reshape((GROUPS, REQUESTS_GROUP)).astype(jnp.int32)
    latent_cache = draw_latent_cache(jax.random.fold_in(keys[7], 71), 0)
    w_q_up = normal_values(keys[4], (QL, HEADS * (NOPE + ROPE)), QL ** -0.5, 0.15625, ((0, 8), (1, 32)))
    w_k_absorb = normal_values(keys[5], (HEADS, NOPE, KVL), NOPE ** -0.5, 0.5, ((0, 32),))
    value_up_weight = normal_values(keys[6], (HEADS, KVL, VD), KVL ** -0.5, 0.25, ((0, 32),))
    return {"q_latent": q_latent, "draft_start": draft_start, "cache_len": cache_len, "latent_cache": latent_cache, "w_q_up": w_q_up, "w_k_absorb": w_k_absorb, "value_up_weight": value_up_weight}


def turn_rotary(query_rope, positions):
    half_width = ROPE // 2
    freqs = 10000.0 ** (-jnp.arange(half_width).astype(jnp.float32) * 2.0 / ROPE)
    angles = positions.astype(jnp.float32)[:, :, None, None] * freqs
    cosine = jnp.cos(angles)
    sine_table = jnp.sin(angles)
    first_half = query_rope[..., :half_width]
    second_half = query_rope[..., half_width:]
    return jnp.concatenate([first_half * cosine - second_half * sine_table, second_half * cosine + first_half * sine_table], axis=-1)


def reference(q_latent, draft_start, cache_len, latent_cache, w_q_up, w_k_absorb, value_up_weight):
    requests = GROUPS * REQUESTS_GROUP
    head_dim = NOPE + ROPE
    flat_rows = q_latent.reshape(requests * DRAFT, QL)
    q_full = jnp.dot(flat_rows, w_q_up, preferred_element_type=jnp.float32).astype(jnp.bfloat16)
    q_full = q_full.reshape(requests, DRAFT, HEADS, head_dim)
    query_nope = q_full[..., :NOPE].astype(jnp.float32)
    query_rope = q_full[..., NOPE:].astype(jnp.float32)
    absorbed = jnp.einsum("rdhn,hnk->rdhk", query_nope, w_k_absorb.astype(jnp.float32), precision=lax.Precision.HIGHEST)
    positions = draft_start.reshape(requests)[:, None] + jnp.arange(DRAFT).astype(jnp.int32)[None, :]
    rotated_rows = turn_rotary(query_rope, positions)
    query = jnp.concatenate([absorbed, rotated_rows], axis=-1).astype(jnp.bfloat16)
    caches = latent_cache.reshape(requests, CTX, KVL + ROPE)
    lengths = cache_len.reshape(requests)
    scale = float(head_dim) ** -0.5

    def one_request(packed):
        request_query, cache, length = packed
        query_matrix = request_query.reshape(DRAFT * HEADS, KVL + ROPE).astype(jnp.float32)
        cache_f = cache.astype(jnp.float32)
        scores = jnp.dot(query_matrix, cache_f.T, precision=lax.Precision.HIGHEST)
        scores = scores.reshape(DRAFT, HEADS, CTX) * scale
        slots = jnp.arange(CTX).astype(jnp.int32)
        limit = length + jnp.arange(DRAFT).astype(jnp.int32)
        visible = slots[None, None, :] <= limit[:, None, None]
        peak = jnp.max(jnp.where(visible, scores, -jnp.inf), axis=2, keepdims=True)
        expo = jnp.where(visible, jnp.exp(scores - peak), 0.0)
        probs = (expo / jnp.sum(expo, axis=2, keepdims=True)).astype(jnp.bfloat16)
        latent_output = jnp.dot(probs.reshape(DRAFT * HEADS, CTX).astype(jnp.float32), cache_f[:, :KVL], precision=lax.Precision.HIGHEST)
        return latent_output.astype(jnp.bfloat16).reshape(DRAFT, HEADS, KVL)

    latent_output = lax.map(one_request, (query, caches, lengths))
    values = jnp.einsum("aofu,fub->aofb", latent_output.astype(jnp.float32), value_up_weight.astype(jnp.float32), precision=lax.Precision.HIGHEST)
    return values.astype(jnp.bfloat16).reshape(GROUPS, REQUESTS_GROUP, DRAFT, HEADS * VD)
```

```python
import functools
import math

import jax
import jax.numpy as jnp
from jax import lax
from jax.experimental import pallas as pl
from jax.experimental.pallas import tpu as pltpu
from jax.sharding import PartitionSpec as P


BF16 = jnp.bfloat16
F32 = jnp.float32
VMEM_LIMIT = 58 << 20
W_CHUNKS = 2
LANES = 128
BLOCK = 512


def ring_gather(chunks, axis_name, size):
    up = [(i, (i + 1) % size) for i in range(size)]
    down = [(i, (i - 1) % size) for i in range(size)]
    half = size // 2
    rows = chunks[0].shape[0]
    ahead, behind = list(chunks), list(chunks)
    pieces = [[(0, chunk)] for chunk in chunks]
    for step in range(1, half + 1):
        for c in range(len(chunks)):
            if step < half:
                ahead[c] = lax.ppermute(ahead[c], axis_name, up)
                behind[c] = lax.ppermute(behind[c], axis_name, down)
                pieces[c] += [(step * rows, ahead[c]), ((size - step) * rows, behind[c])]
            else:
                first = lax.ppermute(ahead[c][: rows // 2], axis_name, up)
                second = lax.ppermute(behind[c][rows // 2 :], axis_name, down)
                pieces[c] += [(step * rows, first), (step * rows + rows // 2, second)]
    return pieces


def query_kernel(offsets, heads, nope, rope, refs):
    n_pieces = len(offsets)
    n_chunks = len(offsets[0])
    q_ref, absorb_ref = refs[0], refs[1]
    flat = sum(len(o) for o in offsets)
    piece_refs = refs[2 : 2 + flat]
    out_ref = refs[2 + flat]
    w_ref, stage_ref, sem = refs[3 + flat :]
    copies = []
    at = 0
    for c, chunk_offsets in enumerate(offsets):
        group = []
        for offset in chunk_offsets:
            source = piece_refs[at]
            copy = pltpu.make_async_copy(
                source, w_ref.at[c, pl.ds(offset, source.shape[0]), :], sem.at[at]
            )
            copy.start()
            group.append(copy)
            at += 1
        copies.append(group)
    rows = q_ref.shape[0] * q_ref.shape[1]
    q = q_ref[...].reshape(rows, q_ref.shape[2])
    per_chunk = heads // len(offsets)
    width = nope + rope
    kv = absorb_ref.shape[2]
    for c, group in enumerate(copies):
        for copy in group:
            copy.wait()
        full = jnp.dot(q, w_ref[c], preferred_element_type=F32).astype(BF16).astype(F32)
        for local in range(per_chunk):
            head = c * per_chunk + local
            start = local * width
            low = full[:, start : start + nope].astype(BF16)
            absorbed = jnp.dot(low, absorb_ref[head], preferred_element_type=F32)
            tail = full[:, start + nope : start + width]
            tail = jnp.concatenate([tail, jnp.zeros((rows, LANES - rope), F32)], axis=1)
            for g in range(kv // LANES):
                stage_ref[g, pl.ds(head, rows, stride=heads), :] = absorbed[
                    :, g * LANES : (g + 1) * LANES
                ]
            stage_ref[kv // LANES, pl.ds(head, rows, stride=heads), :] = tail
    owned, group = out_ref.shape[1:3]
    for g in range(kv // LANES):
        out_ref[..., g * LANES : (g + 1) * LANES] = (
            stage_ref[g].astype(BF16).reshape(-1, owned, group, LANES)
        )
    out_ref[..., kv:] = stage_ref[kv // LANES, :, :rope].astype(BF16).reshape(-1, owned, group, rope)


def build_query(q_all, pieces, absorb, rope, drafts, owned):
    offsets = tuple(tuple(offset for offset, _ in chunk) for chunk in pieces)
    flat = [piece for chunk in pieces for _, piece in chunk]
    heads, nope, kv = absorb.shape
    senders = q_all.shape[0]
    rows = q_all.shape[0] * q_all.shape[1]
    vmem = pl.BlockSpec(memory_space=pltpu.VMEM)
    hbm = pl.BlockSpec(memory_space=pl.ANY)

    def kernel(*refs):
        query_kernel(offsets, heads, nope, rope, refs)

    return pl.pallas_call(
        kernel,
        out_shape=jax.ShapeDtypeStruct((senders, owned, drafts * heads, kv + rope), BF16),
        in_specs=[vmem, vmem] + [hbm] * len(flat),
        out_specs=vmem,
        scratch_shapes=[
            pltpu.VMEM((len(pieces), q_all.shape[2], pieces[0][0][1].shape[1]), BF16),
            pltpu.VMEM((kv // LANES + 1, rows * heads, LANES), F32),
            pltpu.SemaphoreType.DMA((len(flat),)),
        ],
        compiler_params=pltpu.CompilerParams(vmem_limit_bytes=VMEM_LIMIT),
        name="build_query",
    )(q_all, absorb, *flat)


def attend_kernel(heads, kv, factor, len_ref, q_ref, cos_ref, sin_ref, cache_ref, out_ref, *scratch):
    key_ref, qm_ref, score_ref, peak_ref, sum_ref, acc_ref, sem = scratch
    senders, owned, group, width = q_ref.shape
    rows = senders * group
    slots = key_ref.shape[1]
    drafts = group // heads
    blocks = slots // BLOCK
    rope = width - kv

    def copy_of(r, b):
        span = pl.ds(b * BLOCK, BLOCK)
        return pltpu.make_async_copy(
            cache_ref.at[0, r, span, :], key_ref.at[r, span, :], sem.at[r, b]
        )

    counts = []
    for r in range(owned):
        length = len_ref[0, r]
        total = (length + drafts - 1) // BLOCK + 1
        counts.append((length, (length + 1) // BLOCK, jnp.minimum(total, blocks)))
        for b in range(blocks):

            @pl.when(b < counts[r][2])
            def _():
                copy_of(r, b).start()

    for r in range(owned):
        length, full_blocks, total = counts[r]
        raw = q_ref[:, r]
        tail = raw[:, :, kv:].astype(F32)
        half = rope // 2
        swapped = jnp.concatenate([tail[..., half:], tail[..., :half]], axis=-1)
        turned = tail * cos_ref[r] + swapped * sin_ref[r]
        qm_ref[:, :kv] = raw[:, :, :kv].reshape(rows, kv)
        qm_ref[:, kv:] = turned.astype(BF16).reshape(rows, rope)
        peak_ref[...] = jnp.full(peak_ref.shape, -jnp.inf, F32)
        sum_ref[...] = jnp.zeros(sum_ref.shape, F32)
        acc_ref[...] = jnp.zeros(acc_ref.shape, F32)
        lanes = peak_ref.shape[1]

        def score_block(b, masked):
            copy_of(r, b).wait()
            start = pl.multiple_of(b * BLOCK, BLOCK)
            scores = lax.dot_general(
                qm_ref[...],
                key_ref[r, pl.ds(start, BLOCK), :],
                (((1,), (1,)), ((), ())),
                preferred_element_type=F32,
            )
            if masked:
                slot = start + lax.broadcasted_iota(jnp.int32, scores.shape, 1)
                row = lax.broadcasted_iota(jnp.int32, scores.shape, 0)
                draft = lax.rem(row, group) // heads
                scores = jnp.where(slot <= length + draft, scores, -jnp.inf)
            score_ref[:, pl.ds(start, BLOCK)] = scores
            best = peak_ref[...]
            for g in range(BLOCK // lanes):
                best = jnp.maximum(best, scores[:, g * lanes : (g + 1) * lanes])
            peak_ref[...] = best

        def plain(b, carry):
            score_block(b, False)
            return carry

        def edge(b, carry):
            score_block(b, True)
            return carry

        lax.fori_loop(0, full_blocks, plain, 0)
        lax.fori_loop(full_blocks, total, edge, 0)
        peak = jnp.max(peak_ref[...], axis=1, keepdims=True) * factor

        def mix_block(b, carry):
            start = pl.multiple_of(b * BLOCK, BLOCK)
            weights = jnp.exp2(score_ref[:, pl.ds(start, BLOCK)] * factor - peak)
            partial = sum_ref[...]
            for g in range(BLOCK // lanes):
                partial = partial + weights[:, g * lanes : (g + 1) * lanes]
            sum_ref[...] = partial
            acc_ref[...] += jnp.dot(
                weights.astype(BF16),
                key_ref[r, pl.ds(start, BLOCK), :kv],
                preferred_element_type=F32,
            )
            return carry

        lax.fori_loop(0, total, mix_block, 0)
        norm = jnp.sum(sum_ref[...], axis=1, keepdims=True)
        out_ref[:, r] = (acc_ref[...] / norm).astype(BF16).reshape(senders, group, kv)


def attend(arrived, cosine, sine, cache, lengths, heads, kv, scale):
    senders, owned, group, width = arrived.shape
    slots = cache.shape[2]
    rows = senders * group
    vmem = pl.BlockSpec(memory_space=pltpu.VMEM)
    return pl.pallas_call(
        functools.partial(attend_kernel, heads, kv, scale * math.log2(math.e)),
        out_shape=jax.ShapeDtypeStruct((senders, owned, group, kv), BF16),
        in_specs=[
            pl.BlockSpec(memory_space=pltpu.SMEM),
            vmem,
            vmem,
            vmem,
            pl.BlockSpec(memory_space=pl.ANY),
        ],
        out_specs=vmem,
        scratch_shapes=[
            pltpu.VMEM((owned, slots, width), BF16),
            pltpu.VMEM((rows, width), BF16),
            pltpu.VMEM((rows, slots), F32),
            pltpu.VMEM((rows, 128), F32),
            pltpu.VMEM((rows, 128), F32),
            pltpu.VMEM((rows, kv), F32),
            pltpu.SemaphoreType.DMA((owned, slots // BLOCK)),
        ],
        compiler_params=pltpu.CompilerParams(vmem_limit_bytes=VMEM_LIMIT),
        name="attend",
    )(lengths, arrived, cosine, sine, cache)


def value_kernel(lat_ref, up_ref, out_ref, stage_ref):
    heads = up_ref.shape[0]
    parts, all_rows, _ = stage_ref.shape
    rows = all_rows // heads
    for g in range(parts):
        stage_ref[g] = lat_ref[..., g * LANES : (g + 1) * LANES].astype(F32).reshape(all_rows, LANES)
    for head in range(heads):
        low = [stage_ref[g, pl.ds(head, rows, stride=heads), :].astype(BF16) for g in range(parts)]
        low = jnp.concatenate(low, axis=1)
        width = up_ref.shape[2]
        out_ref[:, head * width : (head + 1) * width] = jnp.dot(
            low, up_ref[head], preferred_element_type=F32
        ).astype(BF16)


def expand_values(latent, up):
    heads, kv, width = up.shape
    rows = latent.shape[0] * latent.shape[1] * latent.shape[2]
    vmem = pl.BlockSpec(memory_space=pltpu.VMEM)
    return pl.pallas_call(
        value_kernel,
        out_shape=jax.ShapeDtypeStruct((rows // heads, heads * width), BF16),
        in_specs=[vmem, vmem],
        out_specs=vmem,
        scratch_shapes=[pltpu.VMEM((kv // LANES, rows, LANES), F32)],
        compiler_params=pltpu.CompilerParams(vmem_limit_bytes=VMEM_LIMIT),
        name="expand_values",
    )(latent, up)


def per_device(
    wide, batch, q_latent, draft_start, cache_len, latent_cache, w_q_up, w_k_absorb, value_up_weight
):
    heads_here, nope_width, kv_width = w_k_absorb.shape
    head_dim = w_q_up.shape[1] // heads_here
    rope_width = head_dim - nope_width
    scale = float(head_dim) ** (-0.5)
    _, owned, drafts, latent = q_latent.shape
    slice_rows = w_q_up.shape[0]
    me = lax.axis_index("batch")

    sliced = q_latent.reshape(owned * drafts, batch, slice_rows)
    doubled = jnp.concatenate([sliced, sliced], axis=1)
    picks = [
        lax.dynamic_slice_in_dim(doubled, me + batch - k, 1, axis=1) for k in range(batch)
    ]
    turned = jnp.concatenate(picks, axis=1).reshape(1, owned * drafts, latent)
    copies = jnp.broadcast_to(turned, (wide, owned * drafts, latent))
    q_all = lax.all_to_all(copies, "wide", split_axis=0, concat_axis=0, tiled=True)

    chunk = w_q_up.shape[1] // W_CHUNKS
    pieces = ring_gather(
        [w_q_up[:, c * chunk : (c + 1) * chunk] for c in range(W_CHUNKS)], "batch", batch
    )
    query = build_query(q_all, pieces, w_k_absorb, rope_width, drafts, owned)
    arrived = lax.all_to_all(query, "wide", split_axis=0, concat_axis=0, tiled=True)

    half = rope_width // 2
    freqs = 10000.0 ** (-jnp.arange(half).astype(F32) * 2.0 / rope_width)
    positions = draft_start[0][:, None] + lax.iota(jnp.int32, drafts)[None, :]
    angles = positions.astype(F32)[:, :, None] * freqs
    cosine, sine = jnp.cos(angles), jnp.sin(angles)
    cosine = jnp.repeat(jnp.concatenate([cosine, cosine], axis=-1), heads_here, axis=1)
    sine = jnp.repeat(jnp.concatenate([-sine, sine], axis=-1), heads_here, axis=1)

    mixed = attend(arrived, cosine, sine, latent_cache, cache_len, heads_here, kv_width, scale)
    returned = lax.all_to_all(mixed, "wide", split_axis=0, concat_axis=0, tiled=True)
    values = expand_values(returned, value_up_weight)
    return values.reshape(1, wide * owned, drafts, values.shape[1])


def solution(mesh):
    in_specs = (
        P("batch", "wide", None, None),
        P("batch", "wide"),
        P("batch", "wide"),
        P("batch", "wide", None, None),
        P("batch", "wide"),
        P("wide", None, None),
        P("wide", None, None),
    )
    out_specs = P("batch", None, None, "wide")
    return jax.shard_map(
        functools.partial(per_device, mesh.shape["wide"], mesh.shape["batch"]),
        mesh=mesh,
        in_specs=in_specs,
        out_specs=out_specs,
        check_vma=False,
    )
```

```python
import functools
import math

import jax
import jax.numpy as jnp
from jax import lax
from jax.experimental import pallas as pl
from jax.experimental.pallas import tpu as pltpu
from jax.sharding import PartitionSpec as P


BF16 = jnp.bfloat16
F32 = jnp.float32
VMEM_LIMIT = 58 << 20
LANES = 128
BLOCK = 2048


def near(x):
    return pltpu.with_memory_space_constraint(x, pltpu.VMEM)


def ring_gather(block, axis_name, size):
    up = [(i, (i + 1) % size) for i in range(size)]
    down = [(i, (i - 1) % size) for i in range(size)]
    half = size // 2
    middle = block.shape[0] // 2
    ahead = behind = block
    pieces = [((0, 0), block)]
    for step in range(1, half + 1):
        last = step == half
        ahead = lax.ppermute(ahead[:middle] if last else ahead, axis_name, up)
        behind = lax.ppermute(behind[middle:] if last else behind, axis_name, down)
        pieces += [((size - step, 0), ahead), ((step, middle if last else 0), behind)]
    return pieces


def query_kernel(layout, heads, nope, rope, owned, me_ref, q_ref, absorb_ref, *refs):
    *piece_refs, out_ref, w_ref, stage_ref = refs
    me = me_ref[0]
    senders, local_rows, depth = q_ref.shape
    rows = senders * local_rows
    width = nope + rope
    kv = absorb_ref.shape[2]
    parts = kv // LANES
    size = piece_refs[0].shape[0]
    for (back, row), piece in zip(layout, piece_refs):
        start = pl.multiple_of(lax.rem(me + back, depth // size) * size + row, 32)
        w_ref[pl.ds(start, piece.shape[0]), :] = piece[...]
    full = jnp.dot(q_ref[...].reshape(rows, depth), w_ref[...], preferred_element_type=F32)
    full = full.astype(BF16).astype(F32)
    for head in range(heads):
        start = head * width
        low = full[:, start : start + nope].astype(BF16)
        absorbed = jnp.dot(low, absorb_ref[head], preferred_element_type=F32)
        tail = full[:, start + nope : start + width]
        for g in range(parts):
            stage_ref[g, pl.ds(head, rows, stride=heads), :] = absorbed[
                :, g * LANES : (g + 1) * LANES
            ]
        stage_ref[parts, pl.ds(head, rows, stride=heads), :] = jnp.concatenate(
            [tail] * owned, axis=1
        )
    each = local_rows * heads
    group = each // owned
    for g in range(parts):
        out_ref[:, g * each : (g + 1) * each, :] = (
            stage_ref[g].astype(BF16).reshape(senders, each, LANES)
        )
    tails = stage_ref[parts].reshape(senders, owned, group, LANES)
    lane = lax.broadcasted_iota(jnp.int32, (senders, group, LANES), 2)
    out_ref[:, parts * each :, :] = jnp.where(lane < rope, tails[:, 0], tails[:, 1]).astype(BF16)


def build_query(me, q_all, pieces, absorb, rope, owned):
    layout = tuple(place for place, _ in pieces)
    flat = [piece for _, piece in pieces]
    heads, nope, kv = absorb.shape
    senders, local_rows, depth = q_all.shape
    rows = senders * local_rows
    vmem = pl.BlockSpec(memory_space=pltpu.VMEM)
    out_rows = local_rows * heads * (kv + rope) // LANES
    return pl.pallas_call(
        functools.partial(query_kernel, layout, heads, nope, rope, owned),
        out_shape=jax.ShapeDtypeStruct((senders, out_rows, LANES), BF16),
        in_specs=[pl.BlockSpec(memory_space=pltpu.SMEM)] + [vmem] * (2 + len(flat)),
        out_specs=vmem,
        scratch_shapes=[
            pltpu.VMEM((depth, flat[0].shape[1]), BF16),
            pltpu.VMEM((kv // LANES + 1, rows * heads, LANES), F32),
        ],
        compiler_params=pltpu.CompilerParams(vmem_limit_bytes=VMEM_LIMIT),
        name="build_query",
    )(me, near(q_all), absorb, *[near(piece) for piece in flat])


def attend_kernel(heads, drafts, kv, rope, factor, len_ref, q_ref, cos_ref, sin_ref, cache_ref, out_ref, *scratch):
    key_ref, qm_ref, score_ref, peak_ref, sum_ref, acc_ref, sem = scratch
    senders = q_ref.shape[0]
    owned, _, slots = key_ref.shape
    group = heads * drafts
    rows = senders * group
    blocks = slots // BLOCK
    parts = kv // LANES
    half = rope // 2

    def copy_of(r, b):
        span = pl.ds(b * BLOCK, BLOCK)
        return pltpu.make_async_copy(
            cache_ref.at[0, r, :, span], key_ref.at[r, :, span], sem.at[r, b]
        )

    limits = []
    for r in range(owned):
        length = len_ref[0, r]
        total = jnp.minimum((length + drafts - 1) // BLOCK + 1, blocks)
        limits.append((length, (length + 1) // BLOCK, total))
        for b in range(blocks):

            @pl.when(b < limits[r][2])
            def _():
                copy_of(r, b).start()

    for r in range(owned):
        length, full_blocks, total = limits[r]
        for g in range(parts):
            first = (g * owned + r) * group
            qm_ref[:, g * LANES : (g + 1) * LANES] = q_ref[:, first : first + group, :].reshape(
                rows, LANES
            )
        tail = q_ref[:, parts * owned * group :, r * rope : (r + 1) * rope].astype(F32)
        swapped = jnp.concatenate([tail[..., half:], tail[..., :half]], axis=-1)
        turned = tail * cos_ref[r] + swapped * sin_ref[r]
        qm_ref[:, kv:] = turned.astype(BF16).reshape(rows, rope)
        peak_ref[...] = jnp.full(peak_ref.shape, -jnp.inf, F32)
        sum_ref[...] = jnp.zeros(sum_ref.shape, F32)
        acc_ref[...] = jnp.zeros(acc_ref.shape, F32)

        def score_block(b, masked):
            copy_of(r, b).wait()
            start = pl.multiple_of(b * BLOCK, BLOCK)
            scores = jnp.dot(
                qm_ref[...], key_ref[r, :, pl.ds(start, BLOCK)], preferred_element_type=F32
            )
            if masked:
                slot = start + lax.broadcasted_iota(jnp.int32, scores.shape, 1)
                row = lax.broadcasted_iota(jnp.int32, scores.shape, 0)
                draft = lax.rem(row, group) // heads
                scores = jnp.where(slot <= length + draft, scores, -jnp.inf)
            score_ref[:, pl.ds(start, BLOCK)] = scores
            best = peak_ref[...]
            for g in range(BLOCK // LANES):
                best = jnp.maximum(best, scores[:, g * LANES : (g + 1) * LANES])
            peak_ref[...] = best

        def plain(b, carry):
            score_block(b, False)
            return carry

        def edge(b, carry):
            score_block(b, True)
            return carry

        lax.fori_loop(0, full_blocks, plain, 0)
        lax.fori_loop(full_blocks, total, edge, 0)
        peak = jnp.max(peak_ref[...], axis=1, keepdims=True) * factor

        def mix_block(b, carry):
            start = pl.multiple_of(b * BLOCK, BLOCK)
            weights = jnp.exp2(score_ref[:, pl.ds(start, BLOCK)] * factor - peak)
            partial = sum_ref[...]
            for g in range(BLOCK // LANES):
                partial = partial + weights[:, g * LANES : (g + 1) * LANES]
            sum_ref[...] = partial
            acc_ref[...] += lax.dot_general(
                weights.astype(BF16),
                key_ref[r, :kv, pl.ds(start, BLOCK)],
                (((1,), (1,)), ((), ())),
                preferred_element_type=F32,
            )
            return carry

        lax.fori_loop(0, total, mix_block, 0)
        norm = jnp.sum(sum_ref[...], axis=1, keepdims=True)
        out_ref[:, r * group : (r + 1) * group, :] = (
            (acc_ref[...] / norm).astype(BF16).reshape(senders, group, kv)
        )


def attend(arrived, cosine, sine, cache, lengths, heads, drafts, kv, rope, scale):
    senders = arrived.shape[0]
    owned, width, slots = cache.shape[1:]
    group = heads * drafts
    rows = senders * group
    vmem = pl.BlockSpec(memory_space=pltpu.VMEM)
    return pl.pallas_call(
        functools.partial(attend_kernel, heads, drafts, kv, rope, scale * math.log2(math.e)),
        out_shape=jax.ShapeDtypeStruct((senders, owned * group, kv), BF16),
        in_specs=[
            pl.BlockSpec(memory_space=pltpu.SMEM),
            vmem,
            vmem,
            vmem,
            pl.BlockSpec(memory_space=pl.ANY),
        ],
        out_specs=vmem,
        scratch_shapes=[
            pltpu.VMEM((owned, width, slots), BF16),
            pltpu.VMEM((rows, width), BF16),
            pltpu.VMEM((rows, slots), F32),
            pltpu.VMEM((rows, LANES), F32),
            pltpu.VMEM((rows, LANES), F32),
            pltpu.VMEM((rows, kv), F32),
            pltpu.SemaphoreType.DMA((owned, slots // BLOCK)),
        ],
        compiler_params=pltpu.CompilerParams(vmem_limit_bytes=VMEM_LIMIT),
        name="attend",
    )(lengths, near(arrived), cosine, sine, cache)


def value_kernel(lat_ref, up_ref, out_ref, stage_ref):
    parts, all_rows, _ = stage_ref.shape
    heads, _, width = up_ref.shape
    rows = all_rows // heads
    for g in range(parts):
        stage_ref[g] = lat_ref[..., g * LANES : (g + 1) * LANES].astype(F32).reshape(all_rows, LANES)
    for head in range(heads):
        low = [stage_ref[g, pl.ds(head, rows, stride=heads), :].astype(BF16) for g in range(parts)]
        low = jnp.concatenate(low, axis=1)
        value = jnp.dot(low, up_ref[head], preferred_element_type=F32)
        out_ref[:, :, head * width : (head + 1) * width] = value.reshape(
            out_ref.shape[0], out_ref.shape[1], width
        ).astype(BF16)


def expand_values(latent, up, drafts):
    heads, kv, width = up.shape
    rows = latent.shape[0] * latent.shape[1]
    vmem = pl.BlockSpec(memory_space=pltpu.VMEM)
    return pl.pallas_call(
        value_kernel,
        out_shape=jax.ShapeDtypeStruct((rows // (heads * drafts), drafts, heads * width), BF16),
        in_specs=[vmem, vmem],
        out_specs=vmem,
        scratch_shapes=[pltpu.VMEM((kv // LANES, rows, LANES), F32)],
        compiler_params=pltpu.CompilerParams(vmem_limit_bytes=VMEM_LIMIT),
        name="expand_values",
    )(near(latent), up)


def per_device(
    wide, batch, q_latent, draft_start, cache_len, latent_cache, w_q_up, w_k_absorb, value_up_weight
):
    heads_here, nope_width, kv_width = w_k_absorb.shape
    head_dim = w_q_up.shape[1] // heads_here
    rope_width = head_dim - nope_width
    scale = float(head_dim) ** (-0.5)
    _, owned, drafts, latent = q_latent.shape
    me = lax.axis_index("batch").astype(jnp.int32).reshape(1)

    pieces = ring_gather(w_q_up, "batch", batch)
    copies = jnp.broadcast_to(
        q_latent.reshape(1, owned * drafts, latent), (wide, owned * drafts, latent)
    )
    q_all = lax.all_to_all(copies, "wide", split_axis=0, concat_axis=0, tiled=True)
    query = build_query(me, q_all, pieces, w_k_absorb, rope_width, owned)
    arrived = lax.all_to_all(query, "wide", split_axis=0, concat_axis=0, tiled=True)

    half = rope_width // 2
    shape = (owned, drafts * heads_here, rope_width)
    lane = lax.broadcasted_iota(jnp.int32, shape, 2)
    draft = lax.broadcasted_iota(jnp.int32, shape, 1) // heads_here
    freqs = 10000.0 ** (-lax.rem(lane, half).astype(F32) * 2.0 / rope_width)
    angles = (draft_start[0][:, None, None] + draft).astype(F32) * freqs
    cosine = jnp.cos(angles)
    sine = jnp.sin(angles) * jnp.where(lane < half, -1.0, 1.0)

    mixed = attend(
        arrived,
        cosine,
        sine,
        jnp.swapaxes(latent_cache, 2, 3),
        cache_len,
        heads_here,
        drafts,
        kv_width,
        rope_width,
        scale,
    )
    returned = lax.all_to_all(mixed, "wide", split_axis=0, concat_axis=0, tiled=True)
    values = expand_values(returned, value_up_weight, drafts)
    return values.reshape(1, wide * owned, drafts, values.shape[2])


def solution(mesh):
    in_specs = (
        P("batch", "wide", None, None),
        P("batch", "wide"),
        P("batch", "wide"),
        P("batch", "wide", None, None),
        P("batch", "wide"),
        P("wide", None, None),
        P("wide", None, None),
    )
    out_specs = P("batch", None, None, "wide")
    return jax.shard_map(
        functools.partial(per_device, mesh.shape["wide"], mesh.shape["batch"]),
        mesh=mesh,
        in_specs=in_specs,
        out_specs=out_specs,
        check_vma=False,
    )
```

```python
import functools
import math

import jax
import jax.numpy as jnp
from jax import lax
from jax.experimental import pallas as pl
from jax.experimental.pallas import tpu as pltpu
from jax.sharding import PartitionSpec as P


BF16 = jnp.bfloat16
F32 = jnp.float32
LANES = 128
BLOCK = 2048


def near(x):
    return pltpu.with_memory_space_constraint(x, pltpu.VMEM)


def ring_gather(block, axis_name, size):
    up = [(i, (i + 1) % size) for i in range(size)]
    down = [(i, (i - 1) % size) for i in range(size)]
    half = size // 2
    middle = block.shape[0] // 2
    spans = ((0, middle), (middle, block.shape[0]))
    ahead = lax.ppermute(block, axis_name, up)
    behind = lax.ppermute(block, axis_name, down)
    pieces = [((0, 0), block), ((size - 1, 0), ahead), ((1, 0), behind)]
    ahead = [ahead[first:last] for first, last in spans]
    behind = [behind[first:last] for first, last in spans]
    for step in range(2, half + 1):
        for c, (first, _) in enumerate(spans):
            if step < half or c == 0:
                ahead[c] = lax.ppermute(ahead[c], axis_name, up)
                pieces.append(((size - step, first), ahead[c]))
            if step < half or c == 1:
                behind[c] = lax.ppermute(behind[c], axis_name, down)
                pieces.append(((step, first), behind[c]))
    return pieces


def query_kernel(layout, heads, nope, rope, owned, me_ref, cos_ref, sin_ref, q_ref, absorb_ref, *refs):
    *piece_refs, out_ref, w_ref, stage_ref = refs
    me = me_ref[0]
    senders, local_rows, depth = q_ref.shape
    rows = senders * local_rows
    width = nope + rope
    kv = absorb_ref.shape[2]
    parts = kv // LANES
    size = piece_refs[0].shape[0]
    for (back, row), piece in zip(layout, piece_refs):
        start = pl.multiple_of(lax.rem(me + back, depth // size) * size + row, 32)
        w_ref[pl.ds(start, piece.shape[0]), :] = piece[...]
    full = jnp.dot(q_ref[...].reshape(rows, depth), w_ref[...], preferred_element_type=F32)
    full = full.astype(BF16).astype(F32)
    for head in range(heads):
        start = head * width
        low = full[:, start : start + nope].astype(BF16)
        absorbed = jnp.dot(low, absorb_ref[head], preferred_element_type=F32)
        tail = full[:, start + nope : start + width]
        for g in range(parts):
            stage_ref[g, pl.ds(head, rows, stride=heads), :] = absorbed[
                :, g * LANES : (g + 1) * LANES
            ]
        stage_ref[parts, pl.ds(head, rows, stride=heads), :] = jnp.concatenate(
            [tail] * owned, axis=1
        )
    each = local_rows * heads
    group = each // owned
    for g in range(parts):
        out_ref[:, g * each : (g + 1) * each, :] = (
            stage_ref[g].astype(BF16).reshape(senders, each, LANES)
        )
    tails = stage_ref[parts].reshape(senders, owned, group, LANES)
    lane = lax.broadcasted_iota(jnp.int32, (senders, group, LANES), 2)
    out_ref[:, parts * each :, :] = jnp.where(lane < rope, tails[:, 0], tails[:, 1]).astype(BF16)


def build_query(me, early, q_all, pieces, absorb, rope, owned):
    layout = tuple(place for place, _ in pieces)
    flat = [piece for _, piece in pieces]
    heads, nope, kv = absorb.shape
    senders, local_rows, depth = q_all.shape
    rows = senders * local_rows
    vmem = pl.BlockSpec(memory_space=pltpu.VMEM)
    out_rows = local_rows * heads * (kv + rope) // LANES
    return pl.pallas_call(
        functools.partial(query_kernel, layout, heads, nope, rope, owned),
        out_shape=pltpu.VMEM((senders, out_rows, LANES), BF16),
        in_specs=[pl.BlockSpec(memory_space=pltpu.SMEM)]
        + [vmem] * (len(early) + 2 + len(flat)),
        out_specs=vmem,
        scratch_shapes=[
            pltpu.VMEM((depth, flat[0].shape[1]), BF16),
            pltpu.VMEM((kv // LANES + 1, rows * heads, LANES), F32),
        ],
        compiler_params=pltpu.CompilerParams(vmem_limit_bytes=24 << 20),
        name="build_query",
    )(me, *[near(table) for table in early], near(q_all), absorb, *[near(piece) for piece in flat])


def attend_kernel(heads, drafts, kv, rope, factor, len_ref, q_ref, cos_ref, sin_ref, cache_ref, out_ref, *scratch):
    key_ref, qm_ref, score_ref, peak_ref, sum_ref, acc_ref, sem = scratch
    senders = q_ref.shape[0]
    owned, _, slots = key_ref.shape
    group = heads * drafts
    rows = senders * group
    blocks = slots // BLOCK
    parts = kv // LANES
    half = rope // 2

    def copy_of(r, b):
        span = pl.ds(b * BLOCK, BLOCK)
        return pltpu.make_async_copy(
            cache_ref.at[0, r, :, span], key_ref.at[r, :, span], sem.at[r, b]
        )

    totals = []
    for r in range(owned):
        totals.append(jnp.minimum((len_ref[0, r] + drafts - 1) // BLOCK + 1, blocks))
        for b in range(blocks):

            @pl.when(b < totals[r])
            def _():
                copy_of(r, b).start()

    for r in range(owned):
        for g in range(parts):
            first = (g * owned + r) * group
            qm_ref[r, :, g * LANES : (g + 1) * LANES] = q_ref[:, first : first + group, :].reshape(
                rows, LANES
            )
        tail = q_ref[:, parts * owned * group :, r * rope : (r + 1) * rope].astype(F32)
        swapped = jnp.concatenate([tail[..., half:], tail[..., :half]], axis=-1)
        turned = tail * cos_ref[r] + swapped * sin_ref[r]
        qm_ref[r, :, kv:] = turned.astype(BF16).reshape(rows, rope)

    for r in range(owned):
        length = len_ref[0, r]
        full_blocks = (length + 1) // BLOCK
        total = totals[r]
        peak_ref[...] = jnp.full(peak_ref.shape, -jnp.inf, F32)
        sum_ref[...] = jnp.zeros(sum_ref.shape, F32)
        acc_ref[...] = jnp.zeros(acc_ref.shape, F32)

        def score_block(b, masked):
            copy_of(r, b).wait()
            start = pl.multiple_of(b * BLOCK, BLOCK)
            scores = jnp.dot(
                qm_ref[r], key_ref[r, :, pl.ds(start, BLOCK)], preferred_element_type=F32
            )
            scores = scores * factor
            if masked:
                slot = start + lax.broadcasted_iota(jnp.int32, scores.shape, 1)
                row = lax.broadcasted_iota(jnp.int32, scores.shape, 0)
                draft = lax.rem(row, group) // heads
                scores = jnp.where(slot <= length + draft, scores, -jnp.inf)
            score_ref[:, pl.ds(start, BLOCK)] = scores
            best = peak_ref[...]
            for g in range(BLOCK // LANES):
                best = jnp.maximum(best, scores[:, g * LANES : (g + 1) * LANES])
            peak_ref[...] = best

        def plain(b, carry):
            score_block(b, False)
            return carry

        def edge(b, carry):
            score_block(b, True)
            return carry

        lax.fori_loop(0, full_blocks, plain, 0)
        lax.fori_loop(full_blocks, total, edge, 0)
        peak = jnp.max(peak_ref[...], axis=1, keepdims=True)

        def mix_block(b, carry):
            start = pl.multiple_of(b * BLOCK, BLOCK)
            weights = jnp.exp2(score_ref[:, pl.ds(start, BLOCK)] - peak)
            partial = sum_ref[...]
            for g in range(BLOCK // LANES):
                partial = partial + weights[:, g * LANES : (g + 1) * LANES]
            sum_ref[...] = partial
            acc_ref[...] += lax.dot_general(
                weights.astype(BF16),
                key_ref[r, :kv, pl.ds(start, BLOCK)],
                (((1,), (1,)), ((), ())),
                preferred_element_type=F32,
            )
            return carry

        lax.fori_loop(0, total, mix_block, 0)
        norm = jnp.sum(sum_ref[...], axis=1, keepdims=True)
        out_ref[:, r * group : (r + 1) * group, :] = (
            (acc_ref[...] / norm).astype(BF16).reshape(senders, group, kv)
        )


def attend(arrived, cosine, sine, cache, lengths, heads, drafts, kv, rope, scale):
    senders = arrived.shape[0]
    owned, width, slots = cache.shape[1:]
    group = heads * drafts
    rows = senders * group
    vmem = pl.BlockSpec(memory_space=pltpu.VMEM)
    return pl.pallas_call(
        functools.partial(attend_kernel, heads, drafts, kv, rope, scale * math.log2(math.e)),
        out_shape=pltpu.VMEM((senders, owned * group, kv), BF16),
        in_specs=[pl.BlockSpec(memory_space=pltpu.SMEM)]
        + [vmem] * 3
        + [pl.BlockSpec(memory_space=pl.ANY)],
        out_specs=vmem,
        scratch_shapes=[
            pltpu.VMEM((owned, width, slots), BF16),
            pltpu.VMEM((owned, rows, width), BF16),
            pltpu.VMEM((rows, slots), F32),
            pltpu.VMEM((rows, LANES), F32),
            pltpu.VMEM((rows, LANES), F32),
            pltpu.VMEM((rows, kv), F32),
            pltpu.SemaphoreType.DMA((owned, slots // BLOCK)),
        ],
        compiler_params=pltpu.CompilerParams(vmem_limit_bytes=48 << 20),
        name="attend",
    )(lengths, near(arrived), near(cosine), near(sine), cache)


def value_kernel(lat_ref, up_ref, out_ref, stage_ref):
    parts, all_rows, _ = stage_ref.shape
    heads, _, width = up_ref.shape
    rows = all_rows // heads
    for g in range(parts):
        stage_ref[g] = lat_ref[..., g * LANES : (g + 1) * LANES].astype(F32).reshape(all_rows, LANES)
    for head in range(heads):
        low = [stage_ref[g, pl.ds(head, rows, stride=heads), :].astype(BF16) for g in range(parts)]
        low = jnp.concatenate(low, axis=1)
        value = jnp.dot(low, up_ref[head], preferred_element_type=F32)
        out_ref[:, :, head * width : (head + 1) * width] = value.reshape(
            out_ref.shape[0], out_ref.shape[1], width
        ).astype(BF16)


def expand_values(latent, up, drafts):
    heads, kv, width = up.shape
    rows = latent.shape[0] * latent.shape[1]
    vmem = pl.BlockSpec(memory_space=pltpu.VMEM)
    return pl.pallas_call(
        value_kernel,
        out_shape=jax.ShapeDtypeStruct((rows // (heads * drafts), drafts, heads * width), BF16),
        in_specs=[vmem, vmem],
        out_specs=vmem,
        scratch_shapes=[pltpu.VMEM((kv // LANES, rows, LANES), F32)],
        compiler_params=pltpu.CompilerParams(vmem_limit_bytes=16 << 20),
        name="expand_values",
    )(near(latent), near(up))


def per_device(
    wide, batch, q_latent, draft_start, cache_len, latent_cache, w_q_up, w_k_absorb, value_up_weight
):
    heads_here, nope_width, kv_width = w_k_absorb.shape
    head_dim = w_q_up.shape[1] // heads_here
    rope_width = head_dim - nope_width
    scale = float(head_dim) ** (-0.5)
    _, owned, drafts, latent = q_latent.shape
    me = lax.axis_index("batch").astype(jnp.int32).reshape(1)

    half = rope_width // 2
    shape = (owned, drafts * heads_here, rope_width)
    lane = lax.broadcasted_iota(jnp.int32, shape, 2)
    draft = lax.broadcasted_iota(jnp.int32, shape, 1) // heads_here
    freqs = 10000.0 ** (-lax.rem(lane, half).astype(F32) * 2.0 / rope_width)
    angles = (draft_start[0][:, None, None] + draft).astype(F32) * freqs
    cosine = jnp.cos(angles)
    sine = jnp.sin(angles) * jnp.where(lane < half, -1.0, 1.0)

    pieces = ring_gather(w_q_up, "batch", batch)
    copies = jnp.broadcast_to(
        q_latent.reshape(1, owned * drafts, latent), (wide, owned * drafts, latent)
    )
    q_all = lax.all_to_all(copies, "wide", split_axis=0, concat_axis=0, tiled=True)
    query = build_query(me, (cosine, sine), q_all, pieces, w_k_absorb, rope_width, owned)
    arrived = lax.all_to_all(query, "wide", split_axis=0, concat_axis=0, tiled=True)

    mixed = attend(
        arrived,
        cosine,
        sine,
        jnp.swapaxes(latent_cache, 2, 3),
        cache_len,
        heads_here,
        drafts,
        kv_width,
        rope_width,
        scale,
    )
    returned = lax.all_to_all(mixed, "wide", split_axis=0, concat_axis=0, tiled=True)
    values = expand_values(returned, value_up_weight, drafts)
    return values.reshape(1, wide * owned, drafts, values.shape[2])


def solution(mesh):
    in_specs = (
        P("batch", "wide", None, None),
        P("batch", "wide"),
        P("batch", "wide"),
        P("batch", "wide", None, None),
        P("batch", "wide"),
        P("wide", None, None),
        P("wide", None, None),
    )
    out_specs = P("batch", None, None, "wide")
    return jax.shard_map(
        functools.partial(per_device, mesh.shape["wide"], mesh.shape["batch"]),
        mesh=mesh,
        in_specs=in_specs,
        out_specs=out_specs,
        check_vma=False,
    )
```

```python
import functools
import math

import jax
import jax.numpy as jnp
from jax import lax
from jax.experimental import pallas as pl
from jax.experimental.pallas import tpu as pltpu
from jax.sharding import PartitionSpec as P


BF16 = jnp.bfloat16
F32 = jnp.float32
LANES = 128
BLOCK = 2048


def near(x):
    return pltpu.with_memory_space_constraint(x, pltpu.VMEM)


def ring_gather(block, axis_name, size):
    up = [(i, (i + 1) % size) for i in range(size)]
    down = [(i, (i - 1) % size) for i in range(size)]
    half = size // 2
    middle = block.shape[0] // 2
    spans = ((0, middle), (middle, block.shape[0]))
    ahead = lax.ppermute(block, axis_name, up)
    behind = lax.ppermute(block, axis_name, down)
    pieces = [((0, 0), block), ((size - 1, 0), ahead), ((1, 0), behind)]
    ahead = [ahead[first:last] for first, last in spans]
    behind = [behind[first:last] for first, last in spans]
    for step in range(2, half + 1):
        for c, (first, _) in enumerate(spans):
            if step < half or c == 0:
                ahead[c] = lax.ppermute(ahead[c], axis_name, up)
                pieces.append(((size - step, first), ahead[c]))
            if step < half or c == 1:
                behind[c] = lax.ppermute(behind[c], axis_name, down)
                pieces.append(((step, first), behind[c]))
    return pieces


def near_part_kernel(layout, me_ref, q_ref, *refs):
    *piece_refs, part_ref, last_ref, w_ref = refs
    me = me_ref[0]
    senders, local_rows, depth = q_ref.shape
    size = piece_refs[0].shape[0]
    count = depth // size
    for (back, row), piece in zip(layout, piece_refs):
        start = pl.multiple_of(lax.rem(me + back, count) * size + row, 32)
        w_ref[pl.ds(start, piece.shape[0]), :] = piece[...]
    missing = lax.rem(me + count // 2, count)
    start = pl.multiple_of(missing * size, 64)
    w_ref[pl.ds(start, size), :] = jnp.zeros((size, w_ref.shape[1]), BF16)
    q = q_ref[...].reshape(senders * local_rows, depth)
    last = q[:, :size]
    for k in range(1, count):
        last = jnp.where(missing == k, q[:, k * size : (k + 1) * size], last)
    last_ref[...] = last
    part_ref[...] = jnp.dot(q, w_ref[...], preferred_element_type=F32)


def near_part(me, q_all, pieces):
    senders, local_rows, depth = q_all.shape
    rows = senders * local_rows
    size, columns = pieces[0][1].shape
    vmem = pl.BlockSpec(memory_space=pltpu.VMEM)
    return pl.pallas_call(
        functools.partial(near_part_kernel, tuple(place for place, _ in pieces)),
        out_shape=[pltpu.VMEM((rows, columns), F32), pltpu.VMEM((rows, size), BF16)],
        in_specs=[pl.BlockSpec(memory_space=pltpu.SMEM)] + [vmem] * (1 + len(pieces)),
        out_specs=[vmem, vmem],
        scratch_shapes=[pltpu.VMEM((depth, columns), BF16)],
        compiler_params=pltpu.CompilerParams(vmem_limit_bytes=16 << 20),
        name="near_part",
    )(me, near(q_all), *[near(piece) for _, piece in pieces])


def query_kernel(heads, nope, rope, owned, local_rows, cos_ref, sin_ref, part_ref, last_ref, top_ref, low_ref, absorb_ref, out_ref, stage_ref):
    rows = part_ref.shape[0]
    senders = rows // local_rows
    width = nope + rope
    kv = absorb_ref.shape[2]
    parts = kv // LANES
    w = jnp.concatenate([top_ref[...], low_ref[...]], axis=0)
    full = part_ref[...] + jnp.dot(last_ref[...], w, preferred_element_type=F32)
    full = full.astype(BF16).astype(F32)
    for head in range(heads):
        start = head * width
        low = full[:, start : start + nope].astype(BF16)
        absorbed = jnp.dot(low, absorb_ref[head], preferred_element_type=F32)
        tail = full[:, start + nope : start + width]
        for g in range(parts):
            stage_ref[g, pl.ds(head, rows, stride=heads), :] = absorbed[
                :, g * LANES : (g + 1) * LANES
            ]
        stage_ref[parts, pl.ds(head, rows, stride=heads), :] = jnp.concatenate(
            [tail] * owned, axis=1
        )
    each = local_rows * heads
    group = each // owned
    for g in range(parts):
        out_ref[:, g * each : (g + 1) * each, :] = (
            stage_ref[g].astype(BF16).reshape(senders, each, LANES)
        )
    tails = stage_ref[parts].reshape(senders, owned, group, LANES)
    lane = lax.broadcasted_iota(jnp.int32, (senders, group, LANES), 2)
    out_ref[:, parts * each :, :] = jnp.where(lane < rope, tails[:, 0], tails[:, 1]).astype(BF16)


def build_query(me, early, q_all, pieces, absorb, rope, owned):
    heads, nope, kv = absorb.shape
    senders, local_rows, _ = q_all.shape
    rows = senders * local_rows
    part, last = near_part(me, q_all, pieces[:-2])
    vmem = pl.BlockSpec(memory_space=pltpu.VMEM)
    out_rows = local_rows * heads * (kv + rope) // LANES
    return pl.pallas_call(
        functools.partial(query_kernel, heads, nope, rope, owned, local_rows),
        out_shape=pltpu.VMEM((senders, out_rows, LANES), BF16),
        in_specs=[vmem] * 7,
        out_specs=vmem,
        scratch_shapes=[pltpu.VMEM((kv // LANES + 1, rows * heads, LANES), F32)],
        compiler_params=pltpu.CompilerParams(vmem_limit_bytes=16 << 20),
        name="build_query",
    )(*[near(x) for x in (*early, part, last, pieces[-2][1], pieces[-1][1])], absorb)


def attend_kernel(heads, drafts, kv, rope, factor, len_ref, q_ref, cos_ref, sin_ref, cache_ref, out_ref, *scratch):
    key_ref, qm_ref, score_ref, peak_ref, sum_ref, acc_ref, sem = scratch
    senders = q_ref.shape[0]
    owned, _, slots = key_ref.shape
    group = heads * drafts
    rows = senders * group
    blocks = slots // BLOCK
    parts = kv // LANES
    half = rope // 2

    def copy_of(r, b):
        span = pl.ds(b * BLOCK, BLOCK)
        return pltpu.make_async_copy(
            cache_ref.at[0, r, :, span], key_ref.at[r, :, span], sem.at[r, b]
        )

    totals = []
    for r in range(owned):
        totals.append(jnp.minimum((len_ref[0, r] + drafts - 1) // BLOCK + 1, blocks))
        for b in range(blocks):

            @pl.when(b < totals[r])
            def _():
                copy_of(r, b).start()

    for r in range(owned):
        for g in range(parts):
            first = (g * owned + r) * group
            qm_ref[r, :, g * LANES : (g + 1) * LANES] = q_ref[:, first : first + group, :].reshape(
                rows, LANES
            )
        tail = q_ref[:, parts * owned * group :, r * rope : (r + 1) * rope].astype(F32)
        swapped = jnp.concatenate([tail[..., half:], tail[..., :half]], axis=-1)
        turned = tail * cos_ref[r] + swapped * sin_ref[r]
        qm_ref[r, :, kv:] = turned.astype(BF16).reshape(rows, rope)

    for r in range(owned):
        length = len_ref[0, r]
        full_blocks = (length + 1) // BLOCK
        total = totals[r]
        peak_ref[...] = jnp.full(peak_ref.shape, -jnp.inf, F32)
        sum_ref[...] = jnp.zeros(sum_ref.shape, F32)
        acc_ref[...] = jnp.zeros(acc_ref.shape, F32)

        def score_block(b, masked):
            copy_of(r, b).wait()
            start = pl.multiple_of(b * BLOCK, BLOCK)
            scores = jnp.dot(
                qm_ref[r], key_ref[r, :, pl.ds(start, BLOCK)], preferred_element_type=F32
            )
            scores = scores * factor
            if masked:
                slot = start + lax.broadcasted_iota(jnp.int32, scores.shape, 1)
                row = lax.broadcasted_iota(jnp.int32, scores.shape, 0)
                draft = lax.rem(row, group) // heads
                scores = jnp.where(slot <= length + draft, scores, -jnp.inf)
            score_ref[:, pl.ds(start, BLOCK)] = scores
            best = peak_ref[...]
            for g in range(BLOCK // LANES):
                best = jnp.maximum(best, scores[:, g * LANES : (g + 1) * LANES])
            peak_ref[...] = best

        def plain(b, carry):
            score_block(b, False)
            return carry

        def edge(b, carry):
            score_block(b, True)
            return carry

        lax.fori_loop(0, full_blocks, plain, 0)
        lax.fori_loop(full_blocks, total, edge, 0)
        peak = jnp.max(peak_ref[...], axis=1, keepdims=True)

        def mix_block(b, carry):
            start = pl.multiple_of(b * BLOCK, BLOCK)
            weights = jnp.exp2(score_ref[:, pl.ds(start, BLOCK)] - peak)
            partial = sum_ref[...]
            for g in range(BLOCK // LANES):
                partial = partial + weights[:, g * LANES : (g + 1) * LANES]
            sum_ref[...] = partial
            acc_ref[...] += lax.dot_general(
                weights.astype(BF16),
                key_ref[r, :kv, pl.ds(start, BLOCK)],
                (((1,), (1,)), ((), ())),
                preferred_element_type=F32,
            )
            return carry

        lax.fori_loop(0, total, mix_block, 0)
        norm = jnp.sum(sum_ref[...], axis=1, keepdims=True)
        out_ref[:, r * group : (r + 1) * group, :] = (
            (acc_ref[...] / norm).astype(BF16).reshape(senders, group, kv)
        )


def attend(arrived, cosine, sine, cache, lengths, heads, drafts, kv, rope, scale):
    senders = arrived.shape[0]
    owned, width, slots = cache.shape[1:]
    group = heads * drafts
    rows = senders * group
    vmem = pl.BlockSpec(memory_space=pltpu.VMEM)
    return pl.pallas_call(
        functools.partial(attend_kernel, heads, drafts, kv, rope, scale * math.log2(math.e)),
        out_shape=pltpu.VMEM((senders, owned * group, kv), BF16),
        in_specs=[pl.BlockSpec(memory_space=pltpu.SMEM)]
        + [vmem] * 3
        + [pl.BlockSpec(memory_space=pl.ANY)],
        out_specs=vmem,
        scratch_shapes=[
            pltpu.VMEM((owned, width, slots), BF16),
            pltpu.VMEM((owned, rows, width), BF16),
            pltpu.VMEM((rows, slots), F32),
            pltpu.VMEM((rows, LANES), F32),
            pltpu.VMEM((rows, LANES), F32),
            pltpu.VMEM((rows, kv), F32),
            pltpu.SemaphoreType.DMA((owned, slots // BLOCK)),
        ],
        compiler_params=pltpu.CompilerParams(vmem_limit_bytes=48 << 20),
        name="attend",
    )(lengths, near(arrived), near(cosine), near(sine), cache)


def value_kernel(lat_ref, up_ref, out_ref, stage_ref):
    parts, all_rows, _ = stage_ref.shape
    heads, _, width = up_ref.shape
    rows = all_rows // heads
    for g in range(parts):
        stage_ref[g] = lat_ref[..., g * LANES : (g + 1) * LANES].astype(F32).reshape(all_rows, LANES)
    for head in range(heads):
        low = [stage_ref[g, pl.ds(head, rows, stride=heads), :].astype(BF16) for g in range(parts)]
        low = jnp.concatenate(low, axis=1)
        value = jnp.dot(low, up_ref[head], preferred_element_type=F32)
        out_ref[:, :, head * width : (head + 1) * width] = value.reshape(
            out_ref.shape[0], out_ref.shape[1], width
        ).astype(BF16)


def expand_values(latent, up, drafts):
    heads, kv, width = up.shape
    rows = latent.shape[0] * latent.shape[1]
    vmem = pl.BlockSpec(memory_space=pltpu.VMEM)
    return pl.pallas_call(
        value_kernel,
        out_shape=jax.ShapeDtypeStruct((rows // (heads * drafts), drafts, heads * width), BF16),
        in_specs=[vmem, vmem],
        out_specs=vmem,
        scratch_shapes=[pltpu.VMEM((kv // LANES, rows, LANES), F32)],
        compiler_params=pltpu.CompilerParams(vmem_limit_bytes=16 << 20),
        name="expand_values",
    )(near(latent), near(up))


def per_device(
    wide, batch, q_latent, draft_start, cache_len, latent_cache, w_q_up, w_k_absorb, value_up_weight
):
    heads_here, nope_width, kv_width = w_k_absorb.shape
    head_dim = w_q_up.shape[1] // heads_here
    rope_width = head_dim - nope_width
    scale = float(head_dim) ** (-0.5)
    _, owned, drafts, latent = q_latent.shape
    me = lax.axis_index("batch").astype(jnp.int32).reshape(1)

    half = rope_width // 2
    shape = (owned, drafts * heads_here, rope_width)
    lane = lax.broadcasted_iota(jnp.int32, shape, 2)
    draft = lax.broadcasted_iota(jnp.int32, shape, 1) // heads_here
    freqs = 10000.0 ** (-lax.rem(lane, half).astype(F32) * 2.0 / rope_width)
    angles = (draft_start[0][:, None, None] + draft).astype(F32) * freqs
    cosine = jnp.cos(angles)
    sine = jnp.sin(angles) * jnp.where(lane < half, -1.0, 1.0)

    pieces = ring_gather(w_q_up, "batch", batch)
    copies = jnp.broadcast_to(
        q_latent.reshape(1, owned * drafts, latent), (wide, owned * drafts, latent)
    )
    q_all = lax.all_to_all(copies, "wide", split_axis=0, concat_axis=0, tiled=True)
    query = build_query(me, (cosine, sine), q_all, pieces, w_k_absorb, rope_width, owned)
    arrived = lax.all_to_all(query, "wide", split_axis=0, concat_axis=0, tiled=True)

    mixed = attend(
        arrived,
        cosine,
        sine,
        jnp.swapaxes(latent_cache, 2, 3),
        cache_len,
        heads_here,
        drafts,
        kv_width,
        rope_width,
        scale,
    )
    returned = lax.all_to_all(mixed, "wide", split_axis=0, concat_axis=0, tiled=True)
    values = expand_values(returned, value_up_weight, drafts)
    return values.reshape(1, wide * owned, drafts, values.shape[2])


def solution(mesh):
    in_specs = (
        P("batch", "wide", None, None),
        P("batch", "wide"),
        P("batch", "wide"),
        P("batch", "wide", None, None),
        P("batch", "wide"),
        P("wide", None, None),
        P("wide", None, None),
    )
    out_specs = P("batch", None, None, "wide")
    return jax.shard_map(
        functools.partial(per_device, mesh.shape["wide"], mesh.shape["batch"]),
        mesh=mesh,
        in_specs=in_specs,
        out_specs=out_specs,
        check_vma=False,
    )
```
